512 devices in a mesh: tm: 64 (over x_lo, z, core), head: 8 (over x_hi, y).
Axes of the slice: x: 4 (x_hi: 2, x_lo: 2; x = x_hi * 2 + x_lo), y: 4, z: 16, core: 2. Of those that a mesh axis runs over, the one named last changes fastest.
Arguments:
- frames: bfloat16 [16384, 1280], P('tm', 'head'), may hold values from -6 to 6
- segment_ids: int32 [16384], replicated, may hold values from 0 to 127, never falling along the last dimension, each value on 1 to 256 neighbouring positions
- ln_gain: float32 [1280], replicated, may hold values from 0.5 to 1.5
- ln_bias: float32 [1280], replicated, may hold values from -1.5 to 1.5
- qkv_weight: bfloat16 [3, 1280, 1024], P(None, None, 'head'), may hold values from -3 to 3
- out_weight: bfloat16 [1024, 1280], P(None, 'head'), may hold values from -0.1875 to 0.1875
- out_bias: float32 [1280], P('head'), may hold values from -2.5 to 2.5
- adapter: bfloat16 [1280, 2560], P('head'), may hold values from -0.15625 to 0.15625
- rms_gain: float32 [2560], replicated, may hold values from 0.25 to 1.75
- x_weight: bfloat16 [2560, 2560], P(None, 'head'), may hold values from -0.125 to 0.125
- bc_weight: bfloat16 [2560, 256], P(None, 'head'), may hold values from -0.125 to 0.125
- decay: float32 [4096, 40], P('tm', 'head'), may hold values from 0 to 1
- skip_gain: float32 [40], P('head'), may hold values from 0.5 to 1.5
Outputs:
- encoded: bfloat16 [16384, 1280], P('tm', 'head')
- mixed: bfloat16 [4096, 2560], P('tm', 'head')
The draws below stay inside these ranges and needn't reach their ends.
Inputs may be any that keep to these rules, and one draw needn't show every extreme that they name: `segment_ids`: segment numbers never fall along the frames; each segment holds 1 to 256 frames and one holds exactly 256.
All inputs are finite; a program needn't handle non-finite values.
Results may differ from the reference program's by a relative error of at most 0.008.
Values may be sent and summed in bfloat16 or wider, within the bound.
No kernel may reach another device: no remote copies, remote signals or barrier semaphores. Data moves between devices by JAX's collectives and lax.ppermute only.
A program may use at most 64 MiB of HBM per device.

```python
import math
import jax
import jax.numpy as jnp
import numpy as np
from jax import lax

D = 1280
EHEADS = 16
EHEAD_DIM = 64
DM = 2560
STATE_LAYER_PAIR = 40
HDIM = 64
NSTATE = 128
WINDOW = 256
TOK_DEV = 64
FRAMES = 16384
ELEMENT_COUNT = 4096
SEGMENTS = 128


def draw_qkv_weight(key, part):
    partitioned_table_rows = jax.random.split(key, 1)
    head_width = EHEADS * EHEAD_DIM
    drawn_base = jnp.clip(jax.random.normal(partitioned_table_rows[0], (3, D, head_width), jnp.float32), -4.0, 4.0) * D ** (-0.5)
    return drawn_base.astype(jnp.bfloat16)


def draw_decay(key, part):
    partitioned_table_rows = jax.random.split(key, 7)
    fast_share = 0.5
    chooser = jax.random.uniform(partitioned_table_rows[0], (STATE_LAYER_PAIR,), jnp.float32)
    fast_rate = jnp.exp(jax.random.uniform(partitioned_table_rows[1], (STATE_LAYER_PAIR,), jnp.float32, math.log(1.0 / 50.0), math.log(1.0 / 30.0)))
    slow_rate = jax.random.uniform(partitioned_table_rows[2], (STATE_LAYER_PAIR,), jnp.float32, 0.05, 0.15) * (math.log(10.0) / ELEMENT_COUNT)
    default_speed = jnp.where(chooser < fast_share, fast_rate, slow_rate)
    block_count = ELEMENT_COUNT // TOK_DEV
    block_factor = jnp.exp(jax.random.uniform(partitioned_table_rows[3], (block_count, 1, STATE_LAYER_PAIR), jnp.float32, -math.log(2.0), math.log(2.0)))
    token_factor = jax.random.uniform(partitioned_table_rows[4], (block_count, TOK_DEV, STATE_LAYER_PAIR), jnp.float32, 0.5, 1.5)
    multiplier = (block_factor * token_factor).reshape(ELEMENT_COUNT, STATE_LAYER_PAIR)
    spike_place = jax.random.randint(partitioned_table_rows[5], (3, STATE_LAYER_PAIR), 0, ELEMENT_COUNT)
    peak_remaining_entries = jax.random.uniform(partitioned_table_rows[6], (3, STATE_LAYER_PAIR), jnp.float32, 0.6, 0.8)
    sequence_indices = jnp.arange(ELEMENT_COUNT, dtype=jnp.int32)[:, None, None]
    peak_identical_test = sequence_indices == spike_place[None]
    remaining_proportion = jnp.prod(jnp.where(peak_identical_test, peak_remaining_entries[None], 1.0), axis=1)
    return (jnp.exp(-default_speed[None, :] * multiplier) * remaining_proportion).astype(jnp.float32)


def levels(key, shape, cuts, least, largest):
    level, own = 1.0, jax.random.fold_in(key, 6)
    for axis_at, parts in cuts:
        steps = jnp.exp(jax.random.uniform(jax.random.fold_in(own, axis_at), (parts,), jnp.float32, least / len(cuts), largest / len(cuts)))
        level = level * jnp.repeat(steps, shape[axis_at] // parts).reshape([-1 if axis == axis_at else 1 for axis in range(len(shape))])
    return level


def profile(count, total, most, skew):
    loads = [(1 << 20) // math.isqrt(rank ** skew) + 1 for rank in range(2, count + 1)]
    rest, counts = total - most - (count - 1), [1] * (count - 1)
    while rest > 0:
        candidates = [i for i in range(count - 1) if counts[i] < most]
        mass, remaining = sum([loads[i] for i in candidates]), rest
        for i in candidates:
            extra = min(most - counts[i], max(1, remaining * loads[i] // mass), rest)
            counts[i] = counts[i] + extra
            rest = rest - extra
    return np.array([most] + counts)


def ragged(stream_key, amount, total, most, skew):
    if amount == 2:
        one = jax.random.randint(stream_key, (), max(1, total - most), min(most, total - 1) + 1)
        return jnp.stack([one, total - one])
    lengths = jnp.asarray(profile(amount, total, most, skew), jnp.int32)
    twos = (amount - 1) // 2
    donor, sink = lengths[1:1 + 2 * twos:2], lengths[2:2 + 2 * twos:2]
    room = jnp.minimum(donor - 1, most - sink)
    moved = jax.random.randint(jax.random.fold_in(stream_key, 1), (twos,), 0, 1 << 20) % (room + 1)
    lengths = lengths.at[1:1 + 2 * twos:2].set(donor - moved).at[2:2 + 2 * twos:2].set(sink + moved)
    return lengths[jax.random.permutation(jax.random.fold_in(stream_key, 2), amount)]


def bell_draw(key, dims, scale, reach, cuts=(), kind=jnp.bfloat16):
    drawn = scale * jax.random.normal(key, dims, jnp.float32)
    if cuts:
        drawn = drawn * levels(key, dims, cuts, -0.22, 0.18)
    return jnp.clip(drawn, -reach, reach).astype(kind)


def setup_inputs(seed: int = 0) -> dict:
    arg_keys = jax.random.split(jax.random.key(seed), 14)
    return {
        "frames": bell_draw(arg_keys[0], (FRAMES, D), 1.0, 6.0, ((0, 64), (1, 8))),
        "segment_ids": jnp.searchsorted(jnp.cumsum(ragged(arg_keys[1], SEGMENTS, FRAMES, WINDOW, 1)), jnp.arange(FRAMES), side="right").astype(jnp.int32),
        "ln_gain": jnp.clip(1.0 + 0.1 * jax.random.normal(arg_keys[2], (D,), jnp.float32), 0.5, 1.5),
        "ln_bias": bell_draw(arg_keys[3], (D,), 0.3, 1.5, (), jnp.float32),
        "qkv_weight": draw_qkv_weight(jax.random.fold_in(arg_keys[13], 71), 0),
        "out_weight": bell_draw(arg_keys[5], (EHEADS * EHEAD_DIM, D), (EHEADS * EHEAD_DIM) ** -0.5, 0.1875, ((1, 8),)),
        "out_bias": bell_draw(arg_keys[6], (D,), 0.5, 2.5, ((0, 8),), jnp.float32),
        "adapter": bell_draw(arg_keys[7], (D, DM), D ** -0.5, 0.15625, ((0, 8),)),
        "rms_gain": jnp.clip(1.0 + 0.15 * jax.random.normal(arg_keys[8], (DM,), jnp.float32), 0.25, 1.75),
        "x_weight": bell_draw(arg_keys[9], (DM, STATE_LAYER_PAIR * HDIM), DM ** -0.5, 0.125, ((1, 8),)),
        "bc_weight": bell_draw(arg_keys[10], (DM, 2 * NSTATE), DM ** -0.5, 0.125, ((1, 8),)),
        "decay": draw_decay(jax.random.fold_in(arg_keys[13], 71), 0),
        "skip_gain": jnp.clip(0.5 + 1.0 * jax.random.uniform(arg_keys[12], (STATE_LAYER_PAIR,), jnp.float32) ** levels(arg_keys[12], (STATE_LAYER_PAIR,), ((0, 8),), -0.2, 0.2), 0.5, 1.5),
    }


EPSILON = 1e-05
HIGHEST = lax.Precision.HIGHEST

def layer_norm(values, gain, offset):
    center_mean = lax.optimization_barrier(jnp.mean(values, axis=-1, keepdims=True))
    spread = lax.optimization_barrier(jnp.mean(jnp.square(values - center_mean), axis=-1, keepdims=True))
    return (values - center_mean) * lax.rsqrt(spread + EPSILON) * gain + offset

def block_terms(inputs, b_in, c_in, decay):
    log_decay = jnp.log(decay)
    cumulative = jnp.cumsum(log_decay, axis=0)
    length = inputs.shape[0]
    sequence_indices = jnp.arange(length, dtype=jnp.int32)
    causal = sequence_indices[:, None] >= sequence_indices[None, :]
    log_gap = cumulative[:, None, :] - cumulative[None, :, :]
    weights = jnp.exp(jnp.where(causal[:, :, None], log_gap, -1e+30))
    driven = inputs * (1.0 - decay)[:, :, None]
    affinity = jnp.dot(c_in, b_in.T, preferred_element_type=jnp.float32)
    within = jnp.einsum('tsh,shp->thp', affinity[:, :, None] * weights, driven, precision=HIGHEST)
    tail_decay = jnp.exp(cumulative[-1][None, :] - cumulative)
    end_state = jnp.einsum('sh,shp,sn->hpn', tail_decay, driven, b_in.astype(jnp.float32), precision=HIGHEST)
    return (within, jnp.exp(cumulative), jnp.exp(cumulative[-1]), end_state)

def attend_block(block_index, queries, keys_pad, values_pad, ids_pad, qblock, heads):
    begin = block_index * qblock
    span_rows = qblock + 2 * WINDOW
    query_rows = lax.dynamic_slice_in_dim(queries, begin, qblock, 0).astype(jnp.float32).reshape(qblock, heads, EHEAD_DIM)
    key_rows = lax.dynamic_slice_in_dim(keys_pad, begin, span_rows, 0).astype(jnp.float32).reshape(span_rows, heads, EHEAD_DIM)
    value_rows = lax.dynamic_slice_in_dim(values_pad, begin, span_rows, 0).astype(jnp.float32).reshape(span_rows, heads, EHEAD_DIM)
    query_ids = lax.dynamic_slice_in_dim(ids_pad, begin + WINDOW, qblock, 0)
    key_ids = lax.dynamic_slice_in_dim(ids_pad, begin, span_rows, 0)
    scores = jnp.einsum('qhe,khe->hqk', query_rows, key_rows) * EHEAD_DIM ** (-0.5)
    allowed = query_ids[:, None] == key_ids[None, :]
    scores = jnp.where(allowed[None], scores, -1e+30)
    peak = lax.optimization_barrier(jnp.max(scores, axis=-1, keepdims=True))
    raised = jnp.exp(scores - peak)
    probs = (raised / lax.optimization_barrier(jnp.sum(raised, axis=-1, keepdims=True))).astype(jnp.bfloat16)
    blended = jnp.einsum('hqk,khe->qhe', probs.astype(jnp.float32), value_rows)
    return blended.astype(jnp.bfloat16).reshape(qblock, heads * EHEAD_DIM)

def reference(frames, segment_ids, ln_gain, ln_bias, qkv_weight, out_weight, out_bias, adapter, rms_gain, x_weight, bc_weight, decay, skip_gain):
    frames_wide = frames.astype(jnp.float32)
    normed = layer_norm(frames_wide, ln_gain, ln_bias).astype(jnp.bfloat16)
    queries = jnp.dot(normed, qkv_weight[0], preferred_element_type=jnp.float32).astype(jnp.bfloat16)
    keys_all = jnp.dot(normed, qkv_weight[1], preferred_element_type=jnp.float32).astype(jnp.bfloat16)
    values_all = jnp.dot(normed, qkv_weight[2], preferred_element_type=jnp.float32).astype(jnp.bfloat16)
    keys_pad = jnp.pad(keys_all, ((WINDOW, WINDOW), (0, 0)))
    values_pad = jnp.pad(values_all, ((WINDOW, WINDOW), (0, 0)))
    ids_pad = jnp.pad(segment_ids, (WINDOW, WINDOW), constant_values=-1)
    qblock = math.gcd(FRAMES, 512)

    def attend(block_index):
        return attend_block(block_index, queries, keys_pad, values_pad, ids_pad, qblock, EHEADS)
    attended = lax.map(attend, jnp.arange(FRAMES // qblock, dtype=jnp.int32)).reshape(FRAMES, EHEADS * EHEAD_DIM)
    attention = jnp.dot(attended, out_weight, preferred_element_type=jnp.float32)
    encoded = (frames_wide + attention + out_bias).astype(jnp.bfloat16)
    pooled = lax.optimization_barrier(jnp.mean(encoded.astype(jnp.float32).reshape(ELEMENT_COUNT, 4, D), axis=1)).astype(jnp.bfloat16)
    projected = jnp.dot(pooled, adapter, preferred_element_type=jnp.float32)
    scaled = (projected * lax.rsqrt(lax.optimization_barrier(jnp.mean(jnp.square(projected), axis=-1, keepdims=True)) + EPSILON) * rms_gain).astype(jnp.bfloat16)
    inputs = jax.nn.silu(jnp.dot(scaled, x_weight, preferred_element_type=jnp.float32)).astype(jnp.bfloat16)
    couplers = jax.nn.silu(jnp.dot(scaled, bc_weight, preferred_element_type=jnp.float32)).astype(jnp.bfloat16)
    block_count = ELEMENT_COUNT // TOK_DEV
    input_blocks = inputs.astype(jnp.float32).reshape(block_count, TOK_DEV, STATE_LAYER_PAIR, HDIM)
    coupler_blocks = couplers.reshape(block_count, TOK_DEV, 2 * NSTATE)
    decay_blocks = decay.reshape(block_count, TOK_DEV, STATE_LAYER_PAIR)

    def advance(carried, block_data):
        block_inputs, block_couplers, block_decay = block_data
        c_rows = block_couplers[:, NSTATE:]
        within, growth, total_decay, end_state = block_terms(block_inputs, block_couplers[:, :NSTATE], c_rows, block_decay)
        from_state = jnp.einsum('tn,hpn->thp', c_rows.astype(jnp.float32), carried, precision=HIGHEST)
        result_rows = within + growth[:, :, None] * from_state + skip_gain[None, :, None] * block_inputs
        next_state = total_decay[:, None, None] * carried + end_state
        return (next_state, result_rows.astype(jnp.bfloat16))
    start_state = jnp.zeros((STATE_LAYER_PAIR, HDIM, NSTATE), jnp.float32)
    final_state, mixed_blocks = lax.scan(advance, start_state, (input_blocks, coupler_blocks, decay_blocks))
    mixed = mixed_blocks.reshape(ELEMENT_COUNT, STATE_LAYER_PAIR * HDIM)
    return (encoded, mixed)
```

```python
import math

import jax
import jax.numpy as jnp
from jax import lax
from jax.sharding import PartitionSpec as P

EHEAD_DIM = 64
HDIM = 64
NSTATE = 128
WINDOW = 256
GROUP = 8

EPSILON = 1e-05
HIGHEST = lax.Precision.HIGHEST


def gather(block, axis, groups=None, count=None):
    count = lax.axis_size(axis) if count is None else count
    copies = jnp.broadcast_to(block[None], (count,) + block.shape)
    return lax.all_to_all(copies, axis, 0, 0, tiled=True, axis_index_groups=groups)


def halo(block):
    count = lax.axis_size("tm")
    forward = [(i, i + 1) for i in range(count - 1)]
    backward = [(i + 1, i) for i in range(count - 1)]
    return lax.ppermute(block, "tm", forward), lax.ppermute(block, "tm", backward)


def block_terms(inputs, b_in, c_in, decay):
    cumulative = jnp.cumsum(jnp.log(decay), axis=0)
    length = inputs.shape[0]
    places = jnp.arange(length, dtype=jnp.int32)
    causal = places[:, None] >= places[None, :]
    log_gap = cumulative[:, None, :] - cumulative[None, :, :]
    weights = jnp.exp(jnp.where(causal[:, :, None], log_gap, -1e30))
    driven = inputs * (1.0 - decay)[:, :, None]
    affinity = jnp.dot(c_in, b_in.T, preferred_element_type=jnp.float32)
    within = jnp.einsum("tsh,shp->thp", affinity[:, :, None] * weights, driven, precision=HIGHEST)
    tail_decay = jnp.exp(cumulative[-1][None, :] - cumulative)
    end_state = jnp.einsum(
        "sh,shp,sn->hpn", tail_decay, driven, b_in.astype(jnp.float32), precision=HIGHEST
    )
    return within, jnp.exp(cumulative), jnp.exp(cumulative[-1]), end_state


def state_before(total_decay, end_state):
    count = lax.axis_size("tm")
    place = lax.axis_index("tm")
    near = [[base + k for k in range(GROUP)] for base in range(0, count, GROUP)]
    far = [[lane + GROUP * k for k in range(count // GROUP)] for lane in range(GROUP)]
    heads, width, states = end_state.shape
    rows = heads * width
    share = rows // GROUP
    lane = place % GROUP
    head_rows = jnp.broadcast_to(
        jnp.pad(total_decay, (0, 8 - heads))[None, :, None], (GROUP, 8, states)
    )
    sent = jnp.concatenate([end_state.reshape(GROUP, share, states), head_rows], axis=1)
    got = lax.all_to_all(sent, "tm", 0, 0, tiled=True, axis_index_groups=near)
    row_head = (lane * share + jnp.arange(share, dtype=jnp.int32)) // width

    def spread(decays):
        out = jnp.zeros((share, states), jnp.float32)
        for h in range(heads):
            out = jnp.where((row_head == h)[:, None], decays[h][None, :], out)
        return out

    state = jnp.zeros((share, states), jnp.float32)
    grown = jnp.ones((8, states), jnp.float32)
    entering, kept = [], []
    for k in range(GROUP):
        entering.append(state)
        kept.append(spread(grown))
        state = spread(got[k, share:]) * state + got[k, :share]
        grown = grown * got[k, share:]
    totals = gather(jnp.concatenate([state, grown], axis=0), "tm", far, count // GROUP)
    before = jnp.zeros((share, states), jnp.float32)
    for k in range(count // GROUP):
        step = spread(totals[k, share:]) * before + totals[k, :share]
        before = jnp.where(k < place // GROUP, step, before)
    back = jnp.stack([entering[k] + kept[k] * before for k in range(GROUP)])
    mine = lax.all_to_all(back, "tm", 0, 0, tiled=True, axis_index_groups=near)
    return mine.reshape(heads, width, states)


def per_device(
    frames,
    segment_ids,
    ln_gain,
    ln_bias,
    qkv_weight,
    out_weight,
    out_bias,
    adapter,
    rms_gain,
    x_weight,
    bc_weight,
    decay,
    skip_gain,
):
    frame_count, share = frames.shape
    margin = WINDOW
    tm_slot = lax.axis_index("tm")
    head_count = lax.axis_size("head")
    gathered = gather(frames, "head").astype(jnp.float32)
    width = head_count * share
    center = jnp.sum(gathered, axis=(0, 2), keepdims=True) / width
    spread = jnp.sum(jnp.square(gathered - center), axis=(0, 2), keepdims=True) / width
    normed = (
        (gathered - center) * lax.rsqrt(spread + EPSILON) * ln_gain.reshape(head_count, 1, share)
        + ln_bias.reshape(head_count, 1, share)
    ).astype(jnp.bfloat16)

    def project(weight):
        parts = weight.reshape(head_count, share, weight.shape[1])
        return jnp.einsum(
            "jfc,jcn->fn", normed, parts, preferred_element_type=jnp.float32
        ).astype(jnp.bfloat16)

    keys_own = project(qkv_weight[1])
    values_own = project(qkv_weight[2])
    joined = jnp.concatenate([keys_own, values_own], axis=1)
    low, high = halo(joined)
    queries = project(qkv_weight[0])
    extended = jnp.concatenate([low, joined, high], axis=0)
    head_width = keys_own.shape[1]
    ids_pad = jnp.pad(segment_ids, (margin, margin), constant_values=-1)
    local_ids = lax.dynamic_slice_in_dim(
        ids_pad, tm_slot * frame_count, frame_count + 2 * margin, 0
    )
    heads_dev = head_width // EHEAD_DIM
    allowed = local_ids[margin : margin + frame_count, None] == local_ids[None, :]
    blended = []
    for h in range(heads_dev):
        cols = slice(h * EHEAD_DIM, (h + 1) * EHEAD_DIM)
        key_rows = extended[:, :head_width][:, cols]
        value_rows = extended[:, head_width:][:, cols]
        scores = jnp.einsum(
            "qe,ke->qk", queries[:, cols], key_rows, preferred_element_type=jnp.float32
        ) * EHEAD_DIM ** (-0.5)
        scores = jnp.where(allowed, scores, -1e30)
        raised = jnp.exp(scores - jnp.max(scores, axis=-1, keepdims=True))
        probs = (raised / jnp.sum(raised, axis=-1, keepdims=True)).astype(jnp.bfloat16)
        blended.append(jnp.dot(probs, value_rows, preferred_element_type=jnp.float32))
    attended = jnp.concatenate(blended, axis=1).astype(jnp.bfloat16)
    attention = jnp.einsum(
        "jfc,jcn->fn",
        gather(attended, "head"),
        out_weight.reshape(head_count, head_width, share),
        preferred_element_type=jnp.float32,
    )
    encoded = (frames.astype(jnp.float32) + attention + out_bias).astype(jnp.bfloat16)
    pooled = jnp.mean(
        encoded.astype(jnp.float32).reshape(frame_count // 4, 4, share), axis=1
    ).astype(jnp.bfloat16)
    partial = jnp.dot(pooled, adapter, preferred_element_type=jnp.float32)
    token_count, model = partial.shape
    chunks = partial.astype(jnp.bfloat16).reshape(head_count, token_count // head_count, model)
    parts = lax.all_to_all(chunks, "head", 0, 0, tiled=True)
    projected = jnp.sum(parts.astype(jnp.float32), axis=0)
    own = (
        projected
        * lax.rsqrt(jnp.mean(jnp.square(projected), axis=1, keepdims=True) + EPSILON)
        * rms_gain
    ).astype(jnp.bfloat16)
    scaled = gather(own, "head").reshape(token_count, model)
    coupler_part = jax.nn.silu(
        jnp.dot(scaled, bc_weight, preferred_element_type=jnp.float32)
    ).astype(jnp.bfloat16)
    couplers = gather(coupler_part, "head")
    couplers = jnp.concatenate([couplers[k] for k in range(head_count)], axis=1)
    inputs = jax.nn.silu(jnp.dot(scaled, x_weight, preferred_element_type=jnp.float32)).astype(
        jnp.bfloat16
    )
    state_heads = inputs.shape[1] // HDIM
    inputs_wide = inputs.astype(jnp.float32).reshape(token_count, state_heads, HDIM)
    c_rows = couplers[:, NSTATE:]
    within, growth, total_decay, end_state = block_terms(
        inputs_wide, couplers[:, :NSTATE], c_rows, decay
    )
    incoming = state_before(total_decay, end_state)
    from_state = jnp.einsum(
        "tn,hpn->thp", c_rows.astype(jnp.float32), incoming, precision=HIGHEST
    )
    result_rows = within + growth[:, :, None] * from_state + skip_gain[None, :, None] * inputs_wide
    mixed = result_rows.astype(jnp.bfloat16).reshape(token_count, state_heads * HDIM)
    return (encoded, mixed)


def solution(mesh):
    placed = (
        P("tm", "head"),
        P(),
        P(),
        P(),
        P(None, None, "head"),
        P(None, "head"),
        P("head"),
        P("head", None),
        P(),
        P(None, "head"),
        P(None, "head"),
        P("tm", "head"),
        P("head"),
    )
    return jax.shard_map(
        per_device,
        mesh=mesh,
        in_specs=placed,
        out_specs=(P("tm", "head"), P("tm", "head")),
        check_vma=False,
    )
```

```python
import functools

import jax
import jax.numpy as jnp
from jax import lax
from jax.experimental import pallas as pl
from jax.experimental.pallas import tpu as pltpu
from jax.sharding import PartitionSpec as P

EHEAD_DIM = 64
HDIM = 64
NSTATE = 128
WINDOW = 256
GROUP = 8
POOL = 4

EPSILON = 1e-05
SMALLEST = 1e-37
HIGHEST = lax.Precision.HIGHEST
BF16 = jnp.bfloat16
F32 = jnp.float32


def shape(dims, kind):
    return jax.ShapeDtypeStruct(dims, kind)


def silu(v):
    return v / (1.0 + jnp.exp(-v))


def dot(a, b, dims=((1,), (0,)), precision=None):
    return lax.dot_general(
        a, b, (dims, ((), ())), preferred_element_type=F32, precision=precision
    )


def swap(copies, axis, groups=None):
    return lax.all_to_all(copies, axis, 0, 0, tiled=True, axis_index_groups=groups)


def copy_kernel(x_ref, out_ref):
    value = x_ref[...]
    for j in range(out_ref.shape[0]):
        out_ref[j] = value


def qkv_kernel(x_ref, gain_ref, bias_ref, weight_ref, q_ref, kv_ref):
    count, _, share = x_ref.shape
    features = count * share
    total = 0.0
    for j in range(count):
        total = total + jnp.sum(x_ref[j].astype(F32), axis=-1, keepdims=True)
    center = total / features
    square = 0.0
    for j in range(count):
        square = square + jnp.sum(
            jnp.square(x_ref[j].astype(F32) - center), axis=-1, keepdims=True
        )
    factor = lax.rsqrt(square / features + EPSILON)
    width = weight_ref.shape[2]
    total = 0.0
    for j in range(count):
        normed = ((x_ref[j].astype(F32) - center) * factor * gain_ref[j] + bias_ref[j]).astype(BF16)
        rows = slice(j * share, (j + 1) * share)
        weight = jnp.concatenate([weight_ref[k, rows, :] for k in range(3)], axis=1)
        total = total + dot(normed, weight)
    rounded = total.astype(BF16)
    q_ref[...] = rounded[:, :width] * BF16(EHEAD_DIM**-0.5)
    kv_ref[...] = rounded[:, width:]


def attend_kernel(q_ref, own_ref, low_ref, high_ref, row_ref, col_ref, out_ref):
    rows = q_ref.shape[0]
    width = q_ref.shape[1]
    pieces = (low_ref, own_ref, high_ref)
    allowed = [
        row_ref[...] == col_ref[:, k * rows : (k + 1) * rows] for k in range(len(pieces))
    ]
    blended = []
    for h in range(width // EHEAD_DIM):
        cols = slice(h * EHEAD_DIM, (h + 1) * EHEAD_DIM)
        vals = slice(width + h * EHEAD_DIM, width + (h + 1) * EHEAD_DIM)
        query = q_ref[:, cols]
        scores = [
            jnp.where(ok, dot(query, piece[:, cols], ((1,), (1,))), -1e30)
            for ok, piece in zip(allowed, pieces)
        ]
        peak = functools.reduce(
            jnp.maximum, [jnp.max(s, axis=-1, keepdims=True) for s in scores]
        )
        raised = [jnp.exp(s - peak) for s in scores]
        total = sum(jnp.sum(r, axis=-1, keepdims=True) for r in raised)
        mixed = sum(dot(r.astype(BF16), piece[:, vals]) for r, piece in zip(raised, pieces))
        blended.append(mixed / total)
    value = jnp.concatenate(blended, axis=1).astype(BF16)
    for j in range(out_ref.shape[0]):
        out_ref[j] = value


def encode_kernel(att_ref, weight_ref, frames_ref, bias_ref, adapter_ref, encoded_ref, part_ref):
    count, rows, width = att_ref.shape
    total = 0.0
    for j in range(0, count, 2):
        both = jnp.concatenate([att_ref[j], att_ref[j + 1]], axis=1)
        total = total + dot(both, weight_ref[j * width : (j + 2) * width, :])
    encoded = (frames_ref[...].astype(F32) + total + bias_ref[...]).astype(BF16)
    encoded_ref[...] = encoded
    tokens = rows // POOL
    token = lax.broadcasted_iota(jnp.int32, (tokens, rows), 0)
    frame = lax.broadcasted_iota(jnp.int32, (tokens, rows), 1)
    inside = (frame >= token * POOL) & (frame < (token + 1) * POOL)
    averaging = jnp.where(inside, 1.0 / POOL, 0.0).astype(BF16)
    pooled = dot(averaging, encoded).astype(BF16)
    part = dot(pooled, adapter_ref[...])
    part_ref[...] = part.reshape(part_ref.shape).astype(BF16)


def scale_kernel(part_ref, gain_ref, out_ref):
    projected = jnp.sum(part_ref[...].astype(F32), axis=0)
    spread = jnp.mean(jnp.square(projected), axis=-1, keepdims=True)
    value = (projected * lax.rsqrt(spread + EPSILON) * gain_ref[...]).astype(BF16)
    for j in range(out_ref.shape[0]):
        out_ref[j] = value


def split_rows(rows):
    first = rows.astype(BF16).astype(F32)
    second = (rows - first).astype(BF16).astype(F32)
    third = rows - first - second
    lanes = lax.broadcasted_iota(jnp.int32, rows.shape, 1)
    return jnp.where(lanes < 32, first, jnp.where(lanes < 64, second, third))


def joined_rows(parts):
    return parts[:, 0:1] + parts[:, 32:33] + parts[:, 64:65]


def state_kernel(
    scaled_ref, weight_ref, coupler_ref, decay_ref, skip_ref, base_ref, grow_ref, c_ref, out_ref
):
    scaled = scaled_ref[...]
    inputs = silu(dot(scaled, weight_ref[...])).astype(BF16).astype(F32)
    couplers = jnp.concatenate([coupler_ref[k] for k in range(coupler_ref.shape[0])], axis=1)
    b_in = couplers[:, :NSTATE]
    c_in = couplers[:, NSTATE:]
    c_ref[...] = c_in
    decay = decay_ref[...]
    tokens, heads = decay.shape
    log_decay = jnp.log(jnp.maximum(decay, SMALLEST))
    late = lax.broadcasted_iota(jnp.int32, (tokens, tokens), 0)
    early = lax.broadcasted_iota(jnp.int32, (tokens, tokens), 1)
    causal = late >= early
    below = jnp.where(causal, 1.0, 0.0)
    cumulative = dot(below, log_decay, precision=HIGHEST)
    across = dot(log_decay, below, ((0,), (1,)), precision=HIGHEST)
    grow_ref[...] = jnp.exp(cumulative)
    affinity = dot(c_in, b_in, ((1,), (1,)))
    b_wide = b_in.astype(F32)
    states, totals = [], []
    for h in range(heads):
        cols = slice(h * HDIM, (h + 1) * HDIM)
        column = cumulative[:, h : h + 1]
        gap = jnp.where(causal, column - across[h : h + 1, :], -1e30)
        own = inputs[:, cols]
        driven = own * (1.0 - decay[:, h : h + 1])
        within = dot(affinity * jnp.exp(gap), driven, precision=HIGHEST)
        base_ref[:, cols] = within + skip_ref[h] * own
        last = cumulative[tokens - 1 : tokens, h : h + 1]
        tail = jnp.exp(last - column)
        states.append(dot(driven * tail, b_wide, ((0,), (0,)), precision=HIGHEST))
        totals.append(jnp.broadcast_to(jnp.exp(last), (1, NSTATE)))
    totals.append(jnp.zeros((8 - heads, NSTATE), F32))
    ends = split_rows(jnp.concatenate(totals, axis=0))
    state = jnp.concatenate(states, axis=0)
    share = state.shape[0] // GROUP
    for j in range(GROUP):
        piece = jnp.concatenate([state[j * share : (j + 1) * share], ends], axis=0)
        out_ref[j] = piece.astype(BF16)


def spread_decay(decays, row_head, heads):
    out = jnp.zeros(row_head.shape, F32)
    for h in range(heads):
        out = jnp.where(row_head == h, decays[h : h + 1, :], out)
    return out


def row_heads(lane, share):
    rows = lane * share + lax.broadcasted_iota(jnp.int32, (share, NSTATE), 0)
    return lax.shift_right_logical(rows, HDIM.bit_length() - 1)


def near_kernel(place_ref, got_ref, out_ref, *, heads):
    share = got_ref.shape[1] - 8
    lane = lax.rem(place_ref[0], GROUP)
    row_head = row_heads(lane, share)
    state = jnp.zeros((share, NSTATE), F32)
    grown = jnp.ones((8, 1), F32)
    for k in range(GROUP):
        piece = got_ref[k].astype(F32)
        ends = joined_rows(piece[share:])
        state = spread_decay(ends, row_head, heads) * state + piece[:share]
        grown = grown * ends
    value = jnp.concatenate(
        [state, split_rows(jnp.broadcast_to(grown, (8, NSTATE)))], axis=0
    ).astype(BF16)
    for j in range(out_ref.shape[0]):
        out_ref[j] = value


def far_kernel(place_ref, got_ref, total_ref, out_ref, *, heads):
    share = got_ref.shape[1] - 8
    lane = lax.rem(place_ref[0], GROUP)
    group = lax.div(place_ref[0], GROUP)
    row_head = row_heads(lane, share)
    before = jnp.zeros((share, NSTATE), F32)
    for k in range(total_ref.shape[0]):
        piece = total_ref[k].astype(F32)
        step = spread_decay(joined_rows(piece[share:]), row_head, heads) * before + piece[:share]
        before = jnp.where(k < group, step, before)
    state = before
    for k in range(GROUP):
        out_ref[k] = state.astype(BF16)
        piece = got_ref[k].astype(F32)
        state = spread_decay(joined_rows(piece[share:]), row_head, heads) * state + piece[:share]


def final_kernel(state_ref, c_ref, base_ref, grow_ref, out_ref):
    rows = state_ref.shape[0] * state_ref.shape[1]
    state = state_ref[...].astype(F32).reshape(rows, NSTATE).astype(BF16)
    carried = dot(c_ref[...], state, ((1,), (1,)))
    for h in range(rows // HDIM):
        cols = slice(h * HDIM, (h + 1) * HDIM)
        value = base_ref[:, cols] + grow_ref[:, h : h + 1] * carried[:, cols]
        out_ref[:, cols] = value.astype(BF16)


SMEM = pl.BlockSpec(memory_space=pltpu.SMEM)
VMEM = pl.BlockSpec(memory_space=pltpu.VMEM)


def per_device(
    frames,
    segment_ids,
    ln_gain,
    ln_bias,
    qkv_weight,
    out_weight,
    out_bias,
    adapter,
    rms_gain,
    x_weight,
    bc_weight,
    decay,
    skip_gain,
):
    frame_count, share = frames.shape
    count = lax.axis_size("tm")
    place = lax.axis_index("tm")
    hosts = lax.axis_size("head")
    head_width = qkv_weight.shape[2]
    model = adapter.shape[1]
    tokens, heads = decay.shape
    per = tokens // hosts

    copies = pl.pallas_call(copy_kernel, out_shape=shape((hosts, frame_count, share), BF16))(frames)
    gathered = swap(copies, "head")
    queries, own = pl.pallas_call(
        qkv_kernel,
        out_shape=(
            shape((frame_count, head_width), BF16),
            shape((frame_count, 2 * head_width), BF16),
        ),
    )(gathered, ln_gain.reshape(hosts, 1, share), ln_bias.reshape(hosts, 1, share), qkv_weight)
    low = lax.ppermute(own, "tm", [(i, i + 1) for i in range(count - 1)])
    high = lax.ppermute(own, "tm", [(i + 1, i) for i in range(count - 1)])
    ids = jnp.pad(segment_ids, (WINDOW, WINDOW), constant_values=-1)
    ids = lax.dynamic_slice_in_dim(ids, place * frame_count, frame_count + 2 * WINDOW, 0)
    attended = pl.pallas_call(
        attend_kernel, out_shape=shape((hosts, frame_count, head_width), BF16)
    )(queries, own, low, high, ids[WINDOW : WINDOW + frame_count, None], ids[None, :])
    encoded, parts = pl.pallas_call(
        encode_kernel,
        out_shape=(shape((frame_count, share), BF16), shape((hosts, per, model), BF16)),
    )(swap(attended, "head"), out_weight, frames, out_bias[None, :], adapter)
    scaled = pl.pallas_call(scale_kernel, out_shape=shape((hosts, per, model), BF16))(
        swap(parts, "head"), rms_gain[None, :]
    )
    scaled = swap(scaled, "head").reshape(tokens, model)
    coupler_part = jax.nn.silu(jnp.dot(scaled, bc_weight, preferred_element_type=F32)).astype(BF16)
    couplers = swap(jnp.broadcast_to(coupler_part[None], (hosts,) + coupler_part.shape), "head")

    rows = heads * HDIM // GROUP
    state_shape = shape((GROUP, rows + 8, NSTATE), BF16)
    base, grow, c_rows, ends = pl.pallas_call(
        state_kernel,
        out_shape=(
            shape((tokens, heads * HDIM), F32),
            shape((tokens, heads), F32),
            shape((tokens, NSTATE), BF16),
            state_shape,
        ),
        in_specs=[VMEM, VMEM, VMEM, VMEM, SMEM],
    )(scaled, x_weight, couplers, decay, skip_gain)
    near = [[first + k for k in range(GROUP)] for first in range(0, count, GROUP)]
    far = [[lane + GROUP * k for k in range(count // GROUP)] for lane in range(GROUP)]
    where = place[None].astype(jnp.int32)
    got = swap(ends, "tm", near)
    totals = pl.pallas_call(
        functools.partial(near_kernel, heads=heads),
        out_shape=shape((count // GROUP, rows + 8, NSTATE), BF16),
        in_specs=[SMEM, VMEM],
    )(where, got)
    entering = pl.pallas_call(
        functools.partial(far_kernel, heads=heads),
        out_shape=shape((GROUP, rows, NSTATE), BF16),
        in_specs=[SMEM, VMEM, VMEM],
    )(where, got, swap(totals, "tm", far))
    mixed = pl.pallas_call(final_kernel, out_shape=shape((tokens, heads * HDIM), BF16))(
        swap(entering, "tm", near), c_rows, base, grow
    )
    return (encoded, mixed)


def solution(mesh):
    placed = (
        P("tm", "head"),
        P(),
        P(),
        P(),
        P(None, None, "head"),
        P(None, "head"),
        P("head"),
        P("head", None),
        P(),
        P(None, "head"),
        P(None, "head"),
        P("tm", "head"),
        P("head"),
    )
    return jax.shard_map(
        per_device,
        mesh=mesh,
        in_specs=placed,
        out_specs=(P("tm", "head"), P("tm", "head")),
        check_vma=False,
    )
```

```python
import functools

import jax
import jax.numpy as jnp
from jax import lax
from jax.experimental import pallas as pl
from jax.experimental.pallas import tpu as pltpu
from jax.sharding import PartitionSpec as P

EHEAD_DIM = 64
HDIM = 64
NSTATE = 128
WINDOW = 256
GROUP = 8
POOL = 4

EPSILON = 1e-05
SMALLEST = 1e-37
HIGHEST = lax.Precision.HIGHEST
BF16 = jnp.bfloat16
F32 = jnp.float32


def shape(dims, kind):
    return jax.ShapeDtypeStruct(dims, kind)


def silu(v):
    return v / (1.0 + jnp.exp(-v))


def dot(a, b, dims=((1,), (0,)), precision=None):
    return lax.dot_general(
        a, b, (dims, ((), ())), preferred_element_type=F32, precision=precision
    )


def swap(copies, axis, groups=None):
    return lax.all_to_all(copies, axis, 0, 0, tiled=True, axis_index_groups=groups)


def copy_kernel(x_ref, out_ref):
    value = x_ref[...]
    for j in range(out_ref.shape[0]):
        out_ref[j] = value


def qkv_kernel(x_ref, gain_ref, bias_ref, weight_ref, q_ref, kv_ref):
    count, share, frames = x_ref.shape
    features = count * share
    wide = x_ref[...].astype(F32).reshape(features, frames)
    center = jnp.sum(wide, axis=0, keepdims=True) / features
    wide = wide - center
    spread = jnp.sum(jnp.square(wide), axis=0, keepdims=True) / features
    normed = (wide * lax.rsqrt(spread + EPSILON) * gain_ref[...] + bias_ref[...]).astype(BF16)
    width = q_ref.shape[0]
    rounded = dot(weight_ref[...], normed).astype(BF16)
    q_ref[...] = rounded[:width] * BF16(EHEAD_DIM**-0.5)
    kv_ref[...] = rounded[width:]


def attend_kernel(place_ref, q_ref, own_ref, low_ref, high_ref, ids_ref, out_ref):
    width, frames = q_ref.shape
    blocks = ids_ref.shape[0]
    place = place_ref[0]
    pieces = (low_ref, own_ref, high_ref)
    mine = ids_ref[pl.ds(place, 1), :]
    allowed = []
    for k in range(3):
        at = place + (k - 1)
        ids = ids_ref[pl.ds(jnp.clip(at, 0, blocks - 1), 1), :]
        ids = jnp.where((at >= 0) & (at < blocks), ids, -1.0)
        column = jnp.broadcast_to(ids, (8, frames)).T[:, 0:1]
        allowed.append(column == mine)
    blended = []
    for h in range(width // EHEAD_DIM):
        keys = slice(h * EHEAD_DIM, (h + 1) * EHEAD_DIM)
        vals = slice(width + h * EHEAD_DIM, width + (h + 1) * EHEAD_DIM)
        query = q_ref[keys, :]
        scores = [
            jnp.where(ok, dot(piece[keys, :], query, ((0,), (0,))), -1e30)
            for ok, piece in zip(allowed, pieces)
        ]
        peak = functools.reduce(
            jnp.maximum, [jnp.max(s, axis=0, keepdims=True) for s in scores]
        )
        raised = [jnp.exp(s - peak) for s in scores]
        total = sum(jnp.sum(r, axis=0, keepdims=True) for r in raised)
        mixed = sum(dot(piece[vals, :], r.astype(BF16)) for r, piece in zip(raised, pieces))
        blended.append(mixed / total)
    value = jnp.concatenate(blended, axis=0).astype(BF16)
    for j in range(out_ref.shape[0]):
        out_ref[j] = value


def encode_kernel(att_ref, weight_ref, frames_ref, bias_ref, adapter_ref, encoded_ref, part_ref):
    count, width, rows = att_ref.shape
    total = dot(weight_ref[...], att_ref[...].reshape(count * width, rows))
    encoded = (frames_ref[...].astype(F32) + total + bias_ref[...]).astype(BF16)
    encoded_ref[...] = encoded
    tokens = rows // POOL
    token = lax.broadcasted_iota(jnp.int32, (tokens, rows), 0)
    frame = lax.broadcasted_iota(jnp.int32, (tokens, rows), 1)
    inside = (frame >= token * POOL) & (frame < (token + 1) * POOL)
    averaging = jnp.where(inside, 1.0 / POOL, 0.0).astype(BF16)
    pooled = dot(averaging, encoded, ((1,), (1,))).astype(BF16)
    part = dot(pooled, adapter_ref[...])
    part_ref[...] = part.reshape(part_ref.shape).astype(BF16)


def scale_kernel(part_ref, gain_ref, out_ref):
    projected = jnp.sum(part_ref[...].astype(F32), axis=0)
    spread = jnp.mean(jnp.square(projected), axis=-1, keepdims=True)
    value = (projected * lax.rsqrt(spread + EPSILON) * gain_ref[...]).astype(BF16)
    for j in range(out_ref.shape[0]):
        out_ref[j] = value


def split_rows(rows):
    first = rows.astype(BF16).astype(F32)
    second = (rows - first).astype(BF16).astype(F32)
    third = rows - first - second
    lanes = lax.broadcasted_iota(jnp.int32, rows.shape, 1)
    return jnp.where(lanes < 32, first, jnp.where(lanes < 64, second, third))


def joined_rows(parts):
    return parts[:, 0:1] + parts[:, 32:33] + parts[:, 64:65]


def twice(wide, narrow, dims=((1,), (0,))):
    first = wide.astype(BF16)
    second = (wide - first.astype(F32)).astype(BF16)
    return dot(first, narrow, dims) + dot(second, narrow, dims)


def state_kernel(
    skip_ref, scaled_ref, weight_ref, coupler_ref, decay_ref, base_ref, grow_ref, c_ref, out_ref
):
    scaled = scaled_ref[...]
    inputs = silu(dot(weight_ref[...], scaled, ((1,), (1,)))).astype(BF16)
    couplers = jnp.concatenate([coupler_ref[k] for k in range(coupler_ref.shape[0])], axis=1)
    b_in = couplers[:, :NSTATE]
    c_in = couplers[:, NSTATE:]
    c_ref[...] = c_in
    decay = decay_ref[...]
    heads, tokens = decay.shape
    log_decay = jnp.log(jnp.maximum(decay, SMALLEST))
    late = lax.broadcasted_iota(jnp.int32, (tokens, tokens), 0)
    early = lax.broadcasted_iota(jnp.int32, (tokens, tokens), 1)
    causal = late >= early
    below = jnp.where(causal, 1.0, 0.0)
    cumulative = dot(below, log_decay, ((1,), (1,)), precision=HIGHEST)
    across = dot(log_decay, below, ((1,), (1,)), precision=HIGHEST)
    grow_ref[...] = jnp.exp(cumulative)
    affinity = dot(c_in, b_in, ((1,), (1,)))
    given = 1.0 - decay
    last = across[:, tokens - 1 : tokens]
    tail = jnp.exp(last - across) * given
    states = []
    for h in range(heads):
        cols = slice(h * HDIM, (h + 1) * HDIM)
        gap = jnp.where(causal, cumulative[:, h : h + 1] - across[h : h + 1, :], -1e30)
        weights = affinity * jnp.exp(gap) * given[h : h + 1, :]
        weights = jnp.where(late == early, weights + skip_ref[h], weights)
        base_ref[:, cols] = twice(weights, inputs[cols, :], ((1,), (1,)))
        driven = inputs[cols, :].astype(F32) * tail[h : h + 1, :]
        states.append(twice(driven, b_in))
    ends = jnp.concatenate([jnp.exp(last), jnp.zeros((8 - heads, 1), F32)], axis=0)
    ends = split_rows(jnp.broadcast_to(ends, (8, NSTATE)))
    state = jnp.concatenate(states, axis=0)
    share = state.shape[0] // GROUP
    for j in range(GROUP):
        piece = jnp.concatenate([state[j * share : (j + 1) * share], ends], axis=0)
        out_ref[j] = piece.astype(BF16)


def spread_decay(decays, row_head, heads):
    out = jnp.zeros(row_head.shape, F32)
    for h in range(heads):
        out = jnp.where(row_head == h, decays[h : h + 1, :], out)
    return out


def row_heads(lane, share):
    rows = lane * share + lax.broadcasted_iota(jnp.int32, (share, NSTATE), 0)
    return lax.shift_right_logical(rows, HDIM.bit_length() - 1)


def near_kernel(place_ref, got_ref, out_ref, *, heads):
    share = got_ref.shape[1] - 8
    lane = lax.rem(place_ref[0], GROUP)
    row_head = row_heads(lane, share)
    state = jnp.zeros((share, NSTATE), F32)
    grown = jnp.ones((8, 1), F32)
    for k in range(GROUP):
        piece = got_ref[k].astype(F32)
        ends = joined_rows(piece[share:])
        state = spread_decay(ends, row_head, heads) * state + piece[:share]
        grown = grown * ends
    value = jnp.concatenate(
        [state, split_rows(jnp.broadcast_to(grown, (8, NSTATE)))], axis=0
    ).astype(BF16)
    for j in range(out_ref.shape[0]):
        out_ref[j] = value


def far_kernel(place_ref, got_ref, total_ref, out_ref, *, heads):
    share = got_ref.shape[1] - 8
    lane = lax.rem(place_ref[0], GROUP)
    group = lax.div(place_ref[0], GROUP)
    row_head = row_heads(lane, share)
    before = jnp.zeros((share, NSTATE), F32)
    for k in range(total_ref.shape[0]):
        piece = total_ref[k].astype(F32)
        step = spread_decay(joined_rows(piece[share:]), row_head, heads) * before + piece[:share]
        before = jnp.where(k < group, step, before)
    state = before
    for k in range(GROUP):
        out_ref[k] = state.astype(BF16)
        piece = got_ref[k].astype(F32)
        state = spread_decay(joined_rows(piece[share:]), row_head, heads) * state + piece[:share]


def final_kernel(state_ref, c_ref, base_ref, grow_ref, out_ref):
    rows = state_ref.shape[0] * state_ref.shape[1]
    state = state_ref[...].astype(F32).reshape(rows, NSTATE).astype(BF16)
    carried = dot(c_ref[...], state, ((1,), (1,)))
    for h in range(rows // HDIM):
        cols = slice(h * HDIM, (h + 1) * HDIM)
        value = base_ref[:, cols] + grow_ref[:, h : h + 1] * carried[:, cols]
        out_ref[:, cols] = value.astype(BF16)


def call(kernel, outs, *operands, scalars=0):
    placed = [
        x if k < scalars else pltpu.with_memory_space_constraint(x, pltpu.VMEM)
        for k, x in enumerate(operands)
    ]
    spaces = [pltpu.SMEM if k < scalars else pltpu.VMEM for k in range(len(operands))]
    many = isinstance(outs[0][0], tuple)
    made = pl.pallas_call(
        kernel,
        out_shape=tuple(pltpu.VMEM(dims, kind) for dims, kind in (outs if many else (outs,))),
        in_specs=[pl.BlockSpec(memory_space=space) for space in spaces],
        out_specs=tuple(pl.BlockSpec(memory_space=pltpu.VMEM) for _ in (outs if many else (outs,))),
        compiler_params=pltpu.CompilerParams(vmem_limit_bytes=24 << 20),
    )(*placed)
    return made if many else made[0]


def per_device(
    frames,
    segment_ids,
    ln_gain,
    ln_bias,
    qkv_weight,
    out_weight,
    out_bias,
    adapter,
    rms_gain,
    x_weight,
    bc_weight,
    decay,
    skip_gain,
):
    frame_count, share = frames.shape
    count = lax.axis_size("tm")
    place = lax.axis_index("tm")
    hosts = lax.axis_size("head")
    features = hosts * share
    head_width = qkv_weight.shape[2]
    model = adapter.shape[1]
    tokens, heads = decay.shape
    per = tokens // hosts
    where = place[None].astype(jnp.int32)

    across = frames.T
    copies = call(copy_kernel, ((hosts, share, frame_count), BF16), across)
    gathered = swap(copies, "head")
    queries, own = call(
        qkv_kernel,
        (((head_width, frame_count), BF16), ((2 * head_width, frame_count), BF16)),
        gathered,
        ln_gain[:, None],
        ln_bias[:, None],
        jnp.transpose(qkv_weight, (0, 2, 1)).reshape(3 * head_width, features),
    )
    low = lax.ppermute(own, "tm", [(i, i + 1) for i in range(count - 1)])
    high = lax.ppermute(own, "tm", [(i + 1, i) for i in range(count - 1)])
    attended = call(
        attend_kernel,
        ((hosts, head_width, frame_count), BF16),
        where,
        queries,
        own,
        low,
        high,
        segment_ids.astype(F32).reshape(count, frame_count),
        scalars=1,
    )
    encoded, parts = call(
        encode_kernel,
        (((share, frame_count), BF16), ((hosts, per, model), BF16)),
        swap(attended, "head"),
        out_weight.T,
        across,
        out_bias[:, None],
        adapter,
    )
    scaled = call(
        scale_kernel, ((hosts, per, model), BF16), swap(parts, "head"), rms_gain[None, :]
    )
    scaled = swap(scaled, "head").reshape(tokens, model)
    coupler_part = jax.nn.silu(jnp.dot(scaled, bc_weight, preferred_element_type=F32)).astype(BF16)
    couplers = swap(jnp.broadcast_to(coupler_part[None], (hosts,) + coupler_part.shape), "head")

    rows = heads * HDIM // GROUP
    base, grow, c_rows, ends = call(
        state_kernel,
        (
            ((tokens, heads * HDIM), F32),
            ((tokens, heads), F32),
            ((tokens, NSTATE), BF16),
            ((GROUP, rows + 8, NSTATE), BF16),
        ),
        skip_gain,
        scaled,
        x_weight.T,
        couplers,
        decay.T,
        scalars=1,
    )
    near = [[first + k for k in range(GROUP)] for first in range(0, count, GROUP)]
    far = [[lane + GROUP * k for k in range(count // GROUP)] for lane in range(GROUP)]
    got = swap(ends, "tm", near)
    totals = call(
        functools.partial(near_kernel, heads=heads),
        ((count // GROUP, rows + 8, NSTATE), BF16),
        where,
        got,
        scalars=1,
    )
    entering = call(
        functools.partial(far_kernel, heads=heads),
        ((GROUP, rows, NSTATE), BF16),
        where,
        got,
        swap(totals, "tm", far),
        scalars=1,
    )
    mixed = call(
        final_kernel, ((tokens, heads * HDIM), BF16), swap(entering, "tm", near), c_rows, base, grow
    )
    return (encoded.T, mixed)


def solution(mesh):
    placed = (
        P("tm", "head"),
        P(),
        P(),
        P(),
        P(None, None, "head"),
        P(None, "head"),
        P("head"),
        P("head", None),
        P(),
        P(None, "head"),
        P(None, "head"),
        P("tm", "head"),
        P("head"),
    )
    return jax.shard_map(
        per_device,
        mesh=mesh,
        in_specs=placed,
        out_specs=(P("tm", "head"), P("tm", "head")),
        check_vma=False,
    )
```

```python
import functools

import jax
import jax.numpy as jnp
from jax import lax
from jax.experimental import pallas as pl
from jax.experimental.pallas import tpu as pltpu
from jax.sharding import PartitionSpec as P


EHEAD_DIM = 64
HDIM = 64
NSTATE = 128
GROUP = 8
POOL = 4

EPSILON = 1e-05
SMALLEST = 1e-37
HIGHEST = lax.Precision.HIGHEST
BF16 = jnp.bfloat16
F32 = jnp.float32


def silu(v):
    return v / (1.0 + jnp.exp(-v))


def dot(a, b, dims=((1,), (0,)), precision=None):
    return lax.dot_general(
        a, b, (dims, ((), ())), preferred_element_type=F32, precision=precision
    )


def swap(copies, axis, groups=None):
    return lax.all_to_all(copies, axis, 0, 0, tiled=True, axis_index_groups=groups)


def trade(block, axis, pairs):
    return lax.ppermute(block, axis, pairs + [(b, a) for a, b in pairs])


def gather_halves(rows, hosts, count):
    for bit in (4, 2, 1):
        pairs = [(i, i ^ bit) for i in range(hosts) if not i & bit]
        theirs = trade(rows, "head", pairs)
        rows = jnp.concatenate([rows, theirs], axis=0)
    return rows, trade(rows, "tm", [(i, i + 1) for i in range(0, count, 2)])


def copy_kernel(x_ref, out_ref):
    value = x_ref[...]
    for j in range(out_ref.shape[0]):
        out_ref[j] = value


def qkv_kernel(x_ref, gain_ref, bias_ref, weight_ref, q_ref, kv_ref):
    count, share, frames = x_ref.shape
    features = count * share
    wide = x_ref[...].astype(F32).reshape(features, frames)
    center = jnp.sum(wide, axis=0, keepdims=True) / features
    wide = wide - center
    spread = jnp.sum(jnp.square(wide), axis=0, keepdims=True) / features
    normed = (wide * lax.rsqrt(spread + EPSILON) * gain_ref[...] + bias_ref[...]).astype(BF16)
    width = q_ref.shape[0]
    rounded = dot(weight_ref[...], normed).astype(BF16)
    q_ref[...] = rounded[:width] * BF16(EHEAD_DIM**-0.5)
    kv_ref[...] = rounded[width:]


def attend_kernel(q_ref, own_ref, chip_ref, core_ref, ids_ref, out_ref):
    width, frames = q_ref.shape
    blocks = ids_ref.shape[0]
    place = lax.axis_index("tm")
    pieces = (chip_ref, own_ref, core_ref)
    mine = ids_ref[pl.ds(place, 1), :]
    side = 1 - 2 * lax.rem(place, 2)
    allowed = []
    for at in (place - side, place, place + side):
        ids = ids_ref[pl.ds(jnp.clip(at, 0, blocks - 1), 1), :]
        ids = jnp.where((at >= 0) & (at < blocks), ids, -1.0)
        column = jnp.broadcast_to(ids, (8, frames)).T[:, 0:1]
        allowed.append(column == mine)
    blended = []
    for h in range(width // EHEAD_DIM):
        keys = slice(h * EHEAD_DIM, (h + 1) * EHEAD_DIM)
        vals = slice(width + h * EHEAD_DIM, width + (h + 1) * EHEAD_DIM)
        query = q_ref[keys, :]
        scores = [
            jnp.where(ok, dot(piece[keys, :], query, ((0,), (0,))), -1e30)
            for ok, piece in zip(allowed, pieces)
        ]
        peak = functools.reduce(
            jnp.maximum, [jnp.max(s, axis=0, keepdims=True) for s in scores]
        )
        raised = [jnp.exp(s - peak) for s in scores]
        total = sum(jnp.sum(r, axis=0, keepdims=True) for r in raised)
        mixed = sum(dot(piece[vals, :], r.astype(BF16)) for r, piece in zip(raised, pieces))
        blended.append(mixed / total)
    value = jnp.concatenate(blended, axis=0).astype(BF16)
    for j in range(out_ref.shape[0]):
        out_ref[j] = value


def encode_kernel(att_ref, weight_ref, frames_ref, bias_ref, adapter_ref, encoded_ref, part_ref):
    count, width, rows = att_ref.shape
    total = dot(weight_ref[...], att_ref[...].reshape(count * width, rows))
    encoded = (frames_ref[...].astype(F32) + total + bias_ref[...]).astype(BF16)
    encoded_ref[...] = encoded
    tokens = rows // POOL
    token = lax.broadcasted_iota(jnp.int32, (tokens, rows), 0)
    frame = lax.broadcasted_iota(jnp.int32, (tokens, rows), 1)
    inside = (frame >= token * POOL) & (frame < (token + 1) * POOL)
    averaging = jnp.where(inside, 1.0 / POOL, 0.0).astype(BF16)
    pooled = dot(averaging, encoded, ((1,), (1,))).astype(BF16)
    part = dot(pooled, adapter_ref[...])
    part_ref[...] = part.reshape(part_ref.shape).astype(BF16)


def scale_kernel(part_ref, gain_ref, out_ref):
    projected = jnp.sum(part_ref[...].astype(F32), axis=0)
    spread = jnp.mean(jnp.square(projected), axis=-1, keepdims=True)
    value = (projected * lax.rsqrt(spread + EPSILON) * gain_ref[...]).astype(BF16)
    for j in range(out_ref.shape[0]):
        out_ref[j] = value


def split_rows(rows):
    first = rows.astype(BF16).astype(F32)
    second = (rows - first).astype(BF16).astype(F32)
    third = rows - first - second
    lanes = lax.broadcasted_iota(jnp.int32, rows.shape, 1)
    return jnp.where(lanes < 32, first, jnp.where(lanes < 64, second, third))


def joined_rows(parts):
    return parts[:, 0:1] + parts[:, 32:33] + parts[:, 64:65]


def twice(wide, narrow, dims=((1,), (0,))):
    first = wide.astype(BF16)
    second = (wide - first.astype(F32)).astype(BF16)
    return dot(first, narrow, dims) + dot(second, narrow, dims)


def decay_kernel(decay_ref, skip_ref, weight_ref, diagonal_ref, tail_ref, grow_ref, ends_ref):
    decay = decay_ref[...]
    heads, tokens = decay.shape
    log_decay = jnp.log(jnp.maximum(decay, SMALLEST))
    late = lax.broadcasted_iota(jnp.int32, (tokens, tokens), 0)
    early = lax.broadcasted_iota(jnp.int32, (tokens, tokens), 1)
    causal = late >= early
    below = jnp.where(causal, 1.0, 0.0)
    cumulative = dot(below, log_decay, ((1,), (1,)), precision=HIGHEST)
    across = dot(log_decay, below, ((1,), (1,)), precision=HIGHEST)
    grow_ref[...] = jnp.exp(cumulative)
    given = 1.0 - decay
    last = across[:, tokens - 1 : tokens]
    tail_ref[...] = jnp.exp(last - across) * given
    for h in range(heads):
        gap = jnp.where(causal, cumulative[:, h : h + 1] - across[h : h + 1, :], -1e30)
        weight_ref[h] = jnp.exp(gap) * given[h : h + 1, :]
        diagonal_ref[h] = jnp.where(late == early, skip_ref[:, h : h + 1], 0.0)
    ends = jnp.concatenate([jnp.exp(last), jnp.zeros((8 - heads, 1), F32)], axis=0)
    ends_ref[...] = split_rows(jnp.broadcast_to(ends, (8, NSTATE)))


def fetch(sources, targets, sems):
    moves = [
        pltpu.make_async_copy(source, target, sems.at[k])
        for k, (source, target) in enumerate(zip(sources, targets))
    ]
    for move in moves:
        move.start()
    return moves


def state_kernel(
    scaled_ref,
    x_ref,
    weight_ref,
    diagonal_ref,
    tail_ref,
    ends_ref,
    far_half_ref,
    far_other_ref,
    base_ref,
    c_ref,
    out_ref,
    half_ref,
    other_ref,
    sems,
):
    moves = fetch((far_half_ref, far_other_ref), (half_ref, other_ref), sems)
    scaled = scaled_ref[...]
    inputs = silu(dot(x_ref[...], scaled, ((1,), (1,)))).astype(BF16)
    for move in moves:
        move.wait()
    mine = silu(dot(scaled, half_ref[...], ((1,), (1,))))
    other = silu(dot(scaled, other_ref[...], ((1,), (1,))))
    odd_core = lax.rem(lax.axis_index("tm"), 2) == 1
    flipped = lax.axis_index("head") >= lax.axis_size("head") // 2
    first = jnp.where(odd_core, other, mine)
    second = jnp.where(odd_core, mine, other)
    step = NSTATE // 8
    lane = lax.broadcasted_iota(jnp.int32, first.shape, 1)
    even = lax.rem(lax.div(lane, step), 2) == 0
    one = jnp.where(even, first, pltpu.roll(second, step, 1))
    two = jnp.where(even, pltpu.roll(first, NSTATE - step, 1), second)
    b_in = jnp.where(flipped, two, one).astype(BF16)
    c_in = jnp.where(flipped, one, two).astype(BF16)
    c_ref[...] = c_in
    affinity = dot(c_in, b_in, ((1,), (1,)))
    states = []
    for h in range(weight_ref.shape[0]):
        cols = slice(h * HDIM, (h + 1) * HDIM)
        weights = affinity * weight_ref[h] + diagonal_ref[h]
        base_ref[:, cols] = twice(weights, inputs[cols, :], ((1,), (1,)))
        driven = inputs[cols, :].astype(F32) * tail_ref[h : h + 1, :]
        states.append(twice(driven, b_in))
    state = jnp.concatenate(states, axis=0)
    share = state.shape[0] // GROUP
    for j in range(GROUP):
        piece = jnp.concatenate([state[j * share : (j + 1) * share], ends_ref[...]], axis=0)
        out_ref[j] = piece.astype(BF16)


def spread_decay(decays, row_head, heads):
    out = jnp.zeros(row_head.shape, F32)
    for h in range(heads):
        out = jnp.where(row_head == h, decays[h : h + 1, :], out)
    return out


def row_heads(lane, share):
    rows = lane * share + lax.broadcasted_iota(jnp.int32, (share, NSTATE), 0)
    return lax.shift_right_logical(rows, HDIM.bit_length() - 1)


def near_kernel(got_ref, out_ref, *, heads):
    share = got_ref.shape[1] - 8
    lane = lax.rem(lax.axis_index("tm"), GROUP)
    row_head = row_heads(lane, share)
    state = jnp.zeros((share, NSTATE), F32)
    grown = jnp.ones((8, 1), F32)
    for k in range(GROUP):
        piece = got_ref[k].astype(F32)
        ends = joined_rows(piece[share:])
        state = spread_decay(ends, row_head, heads) * state + piece[:share]
        grown = grown * ends
    value = jnp.concatenate(
        [state, split_rows(jnp.broadcast_to(grown, (8, NSTATE)))], axis=0
    ).astype(BF16)
    for j in range(out_ref.shape[0]):
        out_ref[j] = value


def far_kernel(got_ref, total_ref, out_ref, *, heads):
    share = got_ref.shape[1] - 8
    lane = lax.rem(lax.axis_index("tm"), GROUP)
    group = lax.div(lax.axis_index("tm"), GROUP)
    row_head = row_heads(lane, share)
    before = jnp.zeros((share, NSTATE), F32)
    for k in range(total_ref.shape[0]):
        piece = total_ref[k].astype(F32)
        step = spread_decay(joined_rows(piece[share:]), row_head, heads) * before + piece[:share]
        before = jnp.where(k < group, step, before)
    state = before
    for k in range(GROUP):
        out_ref[k] = state.astype(BF16)
        piece = got_ref[k].astype(F32)
        state = spread_decay(joined_rows(piece[share:]), row_head, heads) * state + piece[:share]


def final_kernel(state_ref, c_ref, base_ref, grow_ref, out_ref):
    rows = state_ref.shape[0] * state_ref.shape[1]
    state = state_ref[...].astype(F32).reshape(rows, NSTATE).astype(BF16)
    carried = dot(c_ref[...], state, ((1,), (1,)))
    for h in range(rows // HDIM):
        cols = slice(h * HDIM, (h + 1) * HDIM)
        value = base_ref[:, cols] + grow_ref[:, h : h + 1] * carried[:, cols]
        out_ref[:, cols] = value.astype(BF16)


def call(kernel, outs, *operands, late=(), final=False):
    vmem = pl.BlockSpec(memory_space=pltpu.VMEM)
    scratch = [pltpu.VMEM(x.shape, x.dtype) for x in late]
    if late:
        scratch.append(pltpu.SemaphoreType.DMA((len(late),)))
    made = pl.pallas_call(
        kernel,
        out_shape=tuple(
            jax.ShapeDtypeStruct(dims, kind) if final else pltpu.VMEM(dims, kind)
            for dims, kind in outs
        ),
        in_specs=[vmem for _ in operands] + [pl.BlockSpec(memory_space=pltpu.HBM) for _ in late],
        out_specs=tuple(vmem for _ in outs),
        scratch_shapes=scratch,
        compiler_params=pltpu.CompilerParams(vmem_limit_bytes=16 << 20),
    )(*[pltpu.with_memory_space_constraint(x, pltpu.VMEM) for x in operands],
        *[pltpu.with_memory_space_constraint(x, pltpu.HBM) for x in late],
    )
    return made if len(outs) > 1 else made[0]


def per_device(
    frames,
    segment_ids,
    ln_gain,
    ln_bias,
    qkv_weight,
    out_weight,
    out_bias,
    adapter,
    rms_gain,
    x_weight,
    bc_weight,
    decay,
    skip_gain,
):
    frame_count, share = frames.shape
    count = lax.axis_size("tm")
    place = lax.axis_index("tm")
    hosts = lax.axis_size("head")
    features = hosts * share
    head_width = qkv_weight.shape[2]
    model = adapter.shape[1]
    tokens, heads = decay.shape
    per = tokens // hosts

    across = frames.T
    copies = call(copy_kernel, (((hosts, share, frame_count), BF16),), across)
    gathered = swap(copies, "head")
    lanes = bc_weight.shape[1] // 2
    half = lax.dynamic_slice_in_dim(bc_weight.T, lax.rem(place, 2) * lanes, lanes, 0)
    half, other = gather_halves(half, hosts, count)
    turned = jnp.transpose(qkv_weight, (0, 2, 1)).reshape(3 * head_width, features)
    queries, own = call(
        qkv_kernel,
        (((head_width, frame_count), BF16), ((2 * head_width, frame_count), BF16)),
        gathered,
        ln_gain[:, None],
        ln_bias[:, None],
        turned,
    )
    chip = trade(own, "tm", [(i, i + 1) for i in range(1, count - 1, 2)])
    core = trade(own, "tm", [(i, i + 1) for i in range(0, count, 2)])
    attended = call(
        attend_kernel,
        (((hosts, head_width, frame_count), BF16),),
        queries,
        own,
        chip,
        core,
        segment_ids.astype(F32).reshape(count, frame_count),
    )
    attended = swap(attended, "head")
    encoded, parts = call(
        encode_kernel,
        (((share, frame_count), BF16), ((hosts, per, model), BF16)),
        attended,
        out_weight.T,
        across,
        out_bias[:, None],
        adapter,
    )
    parts = swap(parts, "head")
    scaled = call(scale_kernel, (((hosts, per, model), BF16),), parts, rms_gain[None, :])
    scaled = swap(scaled, "head")
    scaled = scaled.reshape(tokens, model)
    rows = heads * HDIM // GROUP
    weights, diagonal, tail, grow, ends = call(
        decay_kernel,
        (
            ((heads, tokens, tokens), F32),
            ((heads, tokens, tokens), F32),
            ((heads, tokens), F32),
            ((tokens, heads), F32),
            ((8, NSTATE), F32),
        ),
        decay.T,
        skip_gain[None, :],
    )
    base, c_rows, ends = call(
        state_kernel,
        (
            ((tokens, heads * HDIM), F32),
            ((tokens, NSTATE), BF16),
            ((GROUP, rows + 8, NSTATE), BF16),
        ),
        scaled,
        x_weight.T,
        weights,
        diagonal,
        tail,
        ends,
        late=(half, other),
    )
    near = [[first + k for k in range(GROUP)] for first in range(0, count, GROUP)]
    far = [[lane + GROUP * k for k in range(count // GROUP)] for lane in range(GROUP)]
    got = swap(ends, "tm", near)
    totals = call(
        functools.partial(near_kernel, heads=heads),
        (((count // GROUP, rows + 8, NSTATE), BF16),),
        got,
    )
    entering = call(
        functools.partial(far_kernel, heads=heads),
        (((GROUP, rows, NSTATE), BF16),),
        got,
        swap(totals, "tm", far),
    )
    mixed = call(
        final_kernel,
        (((tokens, heads * HDIM), BF16),),
        swap(entering, "tm", near),
        c_rows,
        base,
        grow,
        final=True,
    )
    return (encoded.T, mixed)


def solution(mesh):
    placed = (
        P("tm", "head"),
        P(),
        P(),
        P(),
        P(None, None, "head"),
        P(None, "head"),
        P("head"),
        P("head", None),
        P(),
        P(None, "head"),
        P(None, "head"),
        P("tm", "head"),
        P("head"),
    )

    return jax.shard_map(
        per_device,
        mesh=mesh,
        in_specs=placed,
        out_specs=(P("tm", "head"), P("tm", "head")),
        check_vma=False,
    )
```

```python
import functools

import jax
import jax.numpy as jnp
from jax import lax
from jax.experimental import pallas as pl
from jax.experimental.pallas import tpu as pltpu
from jax.sharding import PartitionSpec as P


EHEAD_DIM = 64
HDIM = 64
NSTATE = 128
GROUP = 8
POOL = 4

EPSILON = 1e-05
SMALLEST = 1e-37
HIGHEST = lax.Precision.HIGHEST
BF16 = jnp.bfloat16
F32 = jnp.float32


def silu(v):
    return v / (1.0 + jnp.exp(-v))


def dot(a, b, dims=((1,), (0,)), precision=None):
    return lax.dot_general(
        a, b, (dims, ((), ())), preferred_element_type=F32, precision=precision
    )


def swap(copies, axis, groups=None):
    return lax.all_to_all(copies, axis, 0, 0, tiled=True, axis_index_groups=groups)


def trade(block, axis, pairs):
    return lax.ppermute(block, axis, pairs + [(b, a) for a, b in pairs])


def gather_halves(rows, hosts, count):
    cores = [(i, i + 1) for i in range(0, count, 2)]

    def across(block, bit):
        return trade(block, "head", [(i, i ^ bit) for i in range(hosts) if not i & bit])

    theirs = across(rows, 4)
    rows = jnp.concatenate([rows, theirs], axis=0)
    near = trade(rows, "tm", cores)
    second = across(rows, 2)
    rows = jnp.concatenate([rows, second], axis=0)
    third = across(rows, 1)
    later = jnp.concatenate([second, third], axis=0)
    return rows, third, near, trade(later, "tm", cores)


def copy_kernel(x_ref, out_ref):
    value = x_ref[...]
    for j in range(out_ref.shape[0]):
        out_ref[j] = value


def qkv_kernel(x_ref, gain_ref, bias_ref, weight_ref, q_ref, kv_ref):
    count, share, frames = x_ref.shape
    features = count * share
    wide = x_ref[...].astype(F32).reshape(features, frames)
    center = jnp.sum(wide, axis=0, keepdims=True) / features
    wide = wide - center
    spread = jnp.sum(jnp.square(wide), axis=0, keepdims=True) / features
    normed = (wide * lax.rsqrt(spread + EPSILON) * gain_ref[...] + bias_ref[...]).astype(BF16)
    width = q_ref.shape[0]
    rounded = dot(weight_ref[...], normed).astype(BF16)
    q_ref[...] = rounded[:width] * BF16(EHEAD_DIM**-0.5)
    kv_ref[...] = rounded[width:]


def attend_kernel(q_ref, own_ref, chip_ref, core_ref, ids_ref, out_ref):
    width, frames = q_ref.shape
    blocks = ids_ref.shape[0]
    place = lax.axis_index("tm")
    pieces = (chip_ref, own_ref, core_ref)
    mine = ids_ref[pl.ds(place, 1), :]
    side = 1 - 2 * lax.rem(place, 2)
    allowed = []
    for at in (place - side, place, place + side):
        ids = ids_ref[pl.ds(jnp.clip(at, 0, blocks - 1), 1), :]
        ids = jnp.where((at >= 0) & (at < blocks), ids, -1.0)
        column = jnp.broadcast_to(ids, (8, frames)).T[:, 0:1]
        allowed.append(column == mine)
    blended = []
    for h in range(width // EHEAD_DIM):
        keys = slice(h * EHEAD_DIM, (h + 1) * EHEAD_DIM)
        vals = slice(width + h * EHEAD_DIM, width + (h + 1) * EHEAD_DIM)
        query = q_ref[keys, :]
        scores = [
            jnp.where(ok, dot(piece[keys, :], query, ((0,), (0,))), -1e30)
            for ok, piece in zip(allowed, pieces)
        ]
        peak = functools.reduce(
            jnp.maximum, [jnp.max(s, axis=0, keepdims=True) for s in scores]
        )
        raised = [jnp.exp(s - peak) for s in scores]
        total = sum(jnp.sum(r, axis=0, keepdims=True) for r in raised)
        mixed = sum(dot(piece[vals, :], r.astype(BF16)) for r, piece in zip(raised, pieces))
        blended.append(mixed / total)
    value = jnp.concatenate(blended, axis=0).astype(BF16)
    for j in range(out_ref.shape[0]):
        out_ref[j] = value


def encode_kernel(att_ref, weight_ref, frames_ref, bias_ref, adapter_ref, encoded_ref, part_ref):
    count, width, rows = att_ref.shape
    total = dot(weight_ref[...], att_ref[...].reshape(count * width, rows))
    encoded = (frames_ref[...].astype(F32) + total + bias_ref[...]).astype(BF16)
    encoded_ref[...] = encoded
    tokens = rows // POOL
    token = lax.broadcasted_iota(jnp.int32, (tokens, rows), 0)
    frame = lax.broadcasted_iota(jnp.int32, (tokens, rows), 1)
    inside = (frame >= token * POOL) & (frame < (token + 1) * POOL)
    averaging = jnp.where(inside, 1.0 / POOL, 0.0).astype(BF16)
    pooled = dot(averaging, encoded, ((1,), (1,))).astype(BF16)
    part = dot(pooled, adapter_ref[...])
    part_ref[...] = part.reshape(part_ref.shape).astype(BF16)


def add_kernel(part_ref, out_ref):
    value = jnp.sum(part_ref[...].astype(F32), axis=0).astype(BF16)
    for j in range(out_ref.shape[0]):
        out_ref[j] = value


def split_rows(rows):
    first = rows.astype(BF16).astype(F32)
    second = (rows - first).astype(BF16).astype(F32)
    third = rows - first - second
    lanes = lax.broadcasted_iota(jnp.int32, rows.shape, 1)
    return jnp.where(lanes < 32, first, jnp.where(lanes < 64, second, third))


def joined_rows(parts):
    return parts[:, 0:1] + parts[:, 32:33] + parts[:, 64:65]


def decay_kernel(
    encoded_ref, decay_ref, skip_ref, written_ref, weight_ref, diagonal_ref, tail_ref, grow_ref, ends_ref
):
    written_ref[...] = encoded_ref[...]
    decay = decay_ref[...]
    heads, tokens = decay.shape
    log_decay = jnp.log(jnp.maximum(decay, SMALLEST))
    late = lax.broadcasted_iota(jnp.int32, (tokens, tokens), 0)
    early = lax.broadcasted_iota(jnp.int32, (tokens, tokens), 1)
    causal = late >= early
    below = jnp.where(causal, 1.0, 0.0)
    cumulative = dot(below, log_decay, ((1,), (1,)), precision=HIGHEST)
    across = dot(log_decay, below, ((1,), (1,)), precision=HIGHEST)
    grow_ref[...] = jnp.exp(cumulative)
    given = 1.0 - decay
    last = across[:, tokens - 1 : tokens]
    tail_ref[...] = jnp.exp(last - across) * given
    for h in range(heads):
        gap = jnp.where(causal, cumulative[:, h : h + 1] - across[h : h + 1, :], -1e30)
        weight_ref[h] = jnp.exp(gap) * given[h : h + 1, :]
        diagonal_ref[h] = jnp.where(late == early, skip_ref[:, h : h + 1], 0.0)
    ends = jnp.concatenate([jnp.exp(last), jnp.zeros((8 - heads, 1), F32)], axis=0)
    ends_ref[...] = split_rows(jnp.broadcast_to(ends, (8, NSTATE)))


def fetch(sources, targets, sems):
    moves = [
        pltpu.make_async_copy(source, target, sems.at[k])
        for k, (source, target) in enumerate(zip(sources, targets))
    ]
    for move in moves:
        move.start()
    return moves


def state_kernel(
    sums_ref,
    gain_ref,
    x_ref,
    weight_ref,
    diagonal_ref,
    tail_ref,
    ends_ref,
    rows_ref,
    third_ref,
    near_ref,
    far_ref,
    base_ref,
    c_ref,
    out_ref,
    half_ref,
    other_ref,
    sems,
):
    targets = []
    for ref, parts in ((half_ref, (rows_ref, third_ref)), (other_ref, (near_ref, far_ref))):
        edge = parts[0].shape[0]
        targets += [ref.at[pl.ds(0, edge)], ref.at[pl.ds(edge, parts[1].shape[0])]]
    moves = fetch((rows_ref, third_ref, near_ref, far_ref), targets, sems)
    count, per, model = sums_ref.shape
    projected = sums_ref[: count // 2].astype(F32) + sums_ref[count // 2 :].astype(F32)
    projected = projected.reshape(count // 2 * per, model)
    spread = jnp.mean(jnp.square(projected), axis=-1, keepdims=True)
    scaled = (projected * lax.rsqrt(spread + EPSILON) * gain_ref[...]).astype(BF16)
    inputs = silu(dot(x_ref[...], scaled, ((1,), (1,)))).astype(BF16)
    for move in moves:
        move.wait()
    mine = silu(dot(half_ref[...], scaled, ((1,), (1,))))
    other = silu(dot(other_ref[...], scaled, ((1,), (1,))))
    odd_core = lax.rem(lax.axis_index("tm"), 2) == 1
    flipped = lax.axis_index("head") >= lax.axis_size("head") // 2
    first = jnp.where(odd_core, other, mine)
    second = jnp.where(odd_core, mine, other)
    step = NSTATE // 8
    row = lax.broadcasted_iota(jnp.int32, first.shape, 0)
    even = lax.rem(lax.div(row, step), 2) == 0
    one = jnp.where(even, first, pltpu.roll(second, step, 0))
    two = jnp.where(even, pltpu.roll(first, NSTATE - step, 0), second)
    b_in = jnp.where(flipped, two, one).T.astype(BF16)
    c_in = jnp.where(flipped, one, two).T.astype(BF16)
    c_ref[...] = c_in
    affinity = dot(c_in, b_in, ((1,), (1,)))
    heads, tokens = tail_ref.shape
    wide = inputs.astype(F32).reshape(heads, HDIM, tokens) * tail_ref[...].reshape(heads, 1, tokens)
    state = dot(wide.reshape(heads * HDIM, tokens).astype(BF16), b_in)
    for h in range(heads):
        cols = slice(h * HDIM, (h + 1) * HDIM)
        weights = (affinity * weight_ref[h] + diagonal_ref[h]).astype(BF16)
        base_ref[:, cols] = dot(weights, inputs[cols, :], ((1,), (1,)))
    share = state.shape[0] // GROUP
    for j in range(GROUP):
        piece = jnp.concatenate([state[j * share : (j + 1) * share], ends_ref[...]], axis=0)
        out_ref[j] = piece.astype(BF16)


def spread_decay(decays, row_head, heads):
    out = jnp.zeros(row_head.shape, F32)
    for h in range(heads):
        out = jnp.where(row_head == h, decays[h : h + 1, :], out)
    return out


def row_heads(lane, share):
    rows = lane * share + lax.broadcasted_iota(jnp.int32, (share, NSTATE), 0)
    return lax.shift_right_logical(rows, HDIM.bit_length() - 1)


def near_kernel(got_ref, out_ref, *, heads):
    share = got_ref.shape[1] - 8
    lane = lax.rem(lax.axis_index("tm"), GROUP)
    row_head = row_heads(lane, share)
    state = jnp.zeros((share, NSTATE), F32)
    grown = jnp.ones((8, 1), F32)
    for k in range(GROUP):
        piece = got_ref[k].astype(F32)
        ends = joined_rows(piece[share:])
        state = spread_decay(ends, row_head, heads) * state + piece[:share]
        grown = grown * ends
    value = jnp.concatenate(
        [state, split_rows(jnp.broadcast_to(grown, (8, NSTATE)))], axis=0
    ).astype(BF16)
    for j in range(out_ref.shape[0]):
        out_ref[j] = value


def far_kernel(got_ref, total_ref, out_ref, *, heads):
    share = got_ref.shape[1] - 8
    lane = lax.rem(lax.axis_index("tm"), GROUP)
    group = lax.div(lax.axis_index("tm"), GROUP)
    row_head = row_heads(lane, share)
    before = jnp.zeros((share, NSTATE), F32)
    for k in range(total_ref.shape[0]):
        piece = total_ref[k].astype(F32)
        step = spread_decay(joined_rows(piece[share:]), row_head, heads) * before + piece[:share]
        before = jnp.where(k < group, step, before)
    state = before
    for k in range(GROUP):
        out_ref[k] = state.astype(BF16)
        piece = got_ref[k].astype(F32)
        state = spread_decay(joined_rows(piece[share:]), row_head, heads) * state + piece[:share]


def final_kernel(state_ref, c_ref, base_ref, grow_ref, out_ref):
    rows = state_ref.shape[0] * state_ref.shape[1]
    state = state_ref[...].astype(F32).reshape(rows, NSTATE).astype(BF16)
    carried = dot(c_ref[...], state, ((1,), (1,)))
    for h in range(rows // HDIM):
        cols = slice(h * HDIM, (h + 1) * HDIM)
        value = base_ref[:, cols] + grow_ref[:, h : h + 1] * carried[:, cols]
        out_ref[:, cols] = value.astype(BF16)


def call(kernel, outs, *operands, late=(), scratch=(), final=0):
    vmem = pl.BlockSpec(memory_space=pltpu.VMEM)
    scratch = [pltpu.VMEM(*buffer) for buffer in scratch]
    if late:
        scratch.append(pltpu.SemaphoreType.DMA((len(late),)))
    made = pl.pallas_call(
        kernel,
        out_shape=tuple(
            jax.ShapeDtypeStruct(dims, kind) if k < final else pltpu.VMEM(dims, kind)
            for k, (dims, kind) in enumerate(outs)
        ),
        in_specs=[vmem for _ in operands] + [pl.BlockSpec(memory_space=pltpu.HBM) for _ in late],
        out_specs=tuple(vmem for _ in outs),
        scratch_shapes=scratch,
        compiler_params=pltpu.CompilerParams(vmem_limit_bytes=16 << 20),
    )(*[pltpu.with_memory_space_constraint(x, pltpu.VMEM) for x in operands],
        *[pltpu.with_memory_space_constraint(x, pltpu.HBM) for x in late],
    )
    return made if len(outs) > 1 else made[0]


def per_device(
    frames,
    segment_ids,
    ln_gain,
    ln_bias,
    qkv_weight,
    out_weight,
    out_bias,
    adapter,
    rms_gain,
    x_weight,
    bc_weight,
    decay,
    skip_gain,
):
    frame_count, share = frames.shape
    count = lax.axis_size("tm")
    place = lax.axis_index("tm")
    hosts = lax.axis_size("head")
    features = hosts * share
    head_width = qkv_weight.shape[2]
    model = adapter.shape[1]
    tokens, heads = decay.shape
    near_hosts = hosts // 2
    per = tokens // near_hosts

    across = frames.T
    copies = call(copy_kernel, (((hosts, share, frame_count), BF16),), across)
    gathered = swap(copies, "head")
    lanes = bc_weight.shape[1] // 2
    half = lax.dynamic_slice_in_dim(bc_weight.T, lax.rem(place, 2) * lanes, lanes, 0)
    coupler_rows = gather_halves(half, hosts, count)
    turned = jnp.transpose(qkv_weight, (0, 2, 1)).reshape(3 * head_width, features)
    queries, own = call(
        qkv_kernel,
        (((head_width, frame_count), BF16), ((2 * head_width, frame_count), BF16)),
        gathered,
        ln_gain[:, None],
        ln_bias[:, None],
        turned,
    )
    chip = trade(own, "tm", [(i, i + 1) for i in range(1, count - 1, 2)])
    core = trade(own, "tm", [(i, i + 1) for i in range(0, count, 2)])
    attended = call(
        attend_kernel,
        (((hosts, head_width, frame_count), BF16),),
        queries,
        own,
        chip,
        core,
        segment_ids.astype(F32).reshape(count, frame_count),
    )
    attended = swap(attended, "head")
    encoded, parts = call(
        encode_kernel,
        (((share, frame_count), BF16), ((near_hosts, per, model), BF16)),
        attended,
        out_weight.T,
        across,
        out_bias[:, None],
        adapter,
    )
    parts = swap(parts, "head", [list(range(i, i + near_hosts)) for i in range(0, hosts, near_hosts)])
    sums = call(add_kernel, (((hosts, per, model), BF16),), parts)
    sums = swap(sums, "head")
    rows = heads * HDIM // GROUP
    written, weights, diagonal, tail, grow, ends = call(
        decay_kernel,
        (
            ((share, frame_count), BF16),
            ((heads, tokens, tokens), F32),
            ((heads, tokens, tokens), F32),
            ((heads, tokens), F32),
            ((tokens, heads), F32),
            ((8, NSTATE), F32),
        ),
        encoded,
        decay.T,
        skip_gain[None, :],
        final=1,
    )
    base, c_rows, ends = call(
        state_kernel,
        (
            ((tokens, heads * HDIM), F32),
            ((tokens, NSTATE), BF16),
            ((GROUP, rows + 8, NSTATE), BF16),
        ),
        sums,
        rms_gain[None, :],
        x_weight.T,
        weights,
        diagonal,
        tail,
        ends,
        late=coupler_rows,
        scratch=(((NSTATE, model), BF16),) * 2,
    )
    near = [[first + k for k in range(GROUP)] for first in range(0, count, GROUP)]
    far = [[lane + GROUP * k for k in range(count // GROUP)] for lane in range(GROUP)]
    got = swap(ends, "tm", near)
    totals = call(
        functools.partial(near_kernel, heads=heads),
        (((count // GROUP, rows + 8, NSTATE), BF16),),
        got,
    )
    entering = call(
        functools.partial(far_kernel, heads=heads),
        (((GROUP, rows, NSTATE), BF16),),
        got,
        swap(totals, "tm", far),
    )
    mixed = call(
        final_kernel,
        (((tokens, heads * HDIM), BF16),),
        swap(entering, "tm", near),
        c_rows,
        base,
        grow,
        final=1,
    )
    return (written.T, mixed)


def solution(mesh):
    placed = (
        P("tm", "head"),
        P(),
        P(),
        P(),
        P(None, None, "head"),
        P(None, "head"),
        P("head"),
        P("head", None),
        P(),
        P(None, "head"),
        P(None, "head"),
        P("tm", "head"),
        P("head"),
    )

    return jax.shard_map(
        per_device,
        mesh=mesh,
        in_specs=placed,
        out_specs=(P("tm", "head"), P("tm", "head")),
        check_vma=False,
    )
```
